128 devices in a mesh: gx: 4 (over x), gy: 32 (over y, z, core).
Axes of the slice: x: 4, y: 4, z: 4, core: 2. Of those that a mesh axis runs over, the one named last changes fastest.
Arguments:
- charge: float32 [192, 256, 128], P('gx', 'gy'), may hold values from -6 to 6
- kernel_fine: float32 [11, 11, 11], replicated, may hold values from -0.15625 to 0.15625
- kernel_mid: float32 [11, 11, 11], replicated, may hold values from -0.125 to 0.125
- kernel_top: float32 [11, 11, 11], replicated, may hold values from -0.0625 to 0.0625
Outputs:
- potential: float32 [192, 256, 128], P('gx', 'gy')
The draws below stay inside these ranges and needn't reach their ends.
All inputs are finite; a program needn't handle non-finite values.
Results may differ from the reference program's by a relative error of at most 0.000073.
Values sent between devices are 32-bit elements; how exact they have to be, the bound alone decides.
A program may use at most 128 MiB of HBM per device.

```python
import jax
import jax.numpy as jnp
from jax import lax

NZ = 128
KW = 11
NX = 192
NY = 256


def draw_charge(key, part):
    rough_key = jax.random.fold_in(key, 11)
    rough = jax.random.normal(rough_key, (NX, NY, NZ), jnp.float32)
    return jnp.clip(rough, -6.0, 6.0)


def noise(key, shape, deviation, limit, held_as=jnp.bfloat16):
    drawn = jax.random.normal(key, shape, jnp.float32) * deviation
    return jnp.minimum(jnp.maximum(drawn, -limit), limit).astype(held_as)


def setup_inputs(seed: int = 0) -> dict:
    splits = jax.random.split(jax.random.key(seed), 5)
    charge = draw_charge(jax.random.fold_in(splits[4], 71), 0)
    kernel_fine = noise(splits[1], (KW, KW, KW), (KW * KW * KW) ** -0.5, 0.15625, jnp.float32)
    kernel_mid = noise(splits[2], (KW, KW, KW), (2 * KW * KW * KW) ** -0.5, 0.125, jnp.float32)
    kernel_top = noise(splits[3], (KW, KW, KW), (8 * KW * KW * KW) ** -0.5, 0.0625, jnp.float32)
    return dict(charge=charge, kernel_fine=kernel_fine, kernel_mid=kernel_mid, kernel_top=kernel_top)


SPLINE = (0.125, 0.5, 0.75, 0.5, 0.125)


def restrict_axis(values, axis):
    half = values.shape[axis] // 2
    widths = [(0, 0), (0, 0), (0, 0)]
    widths[axis] = (2, 2)
    padded = jnp.pad(values, widths)
    total = None
    for place, weight in enumerate(SPLINE):
        piece = lax.slice_in_dim(padded, place, place + 2 * half - 1, 2, axis)
        total = weight * piece if total is None else total + weight * piece
    return total


def restrict(values):
    for axis in range(3):
        values = restrict_axis(values, axis)
    return values


def prolong_axis(values, axis):
    count = values.shape[axis] - 2
    before = lax.slice_in_dim(values, 0, count, 1, axis)
    centre = lax.slice_in_dim(values, 1, count + 1, 1, axis)
    after = lax.slice_in_dim(values, 2, count + 2, 1, axis)
    even = 0.125 * before + 0.75 * centre + 0.125 * after
    odd = 0.5 * centre + 0.5 * after
    target = list(values.shape)
    target[axis] = 2 * count
    return jnp.stack([even, odd], axis=axis + 1).reshape(target)


def prolong(values):
    for axis in range(3):
        widths = [(0, 0), (0, 0), (0, 0)]
        widths[axis] = (1, 1)
        values = prolong_axis(jnp.pad(values, widths), axis)
    return values


def convolve(field, kernel):
    radius = kernel.shape[0] // 2
    lengths = tuple(extent + 2 * radius for extent in field.shape)
    flipped = kernel[::-1, ::-1, ::-1]
    spectrum = jnp.fft.rfftn(field, lengths) * jnp.fft.rfftn(flipped, lengths)
    full = jnp.fft.irfftn(spectrum, lengths)
    return full[radius:radius + field.shape[0], radius:radius + field.shape[1], radius:radius + field.shape[2]]


def reference(charge, kernel_fine, kernel_mid, kernel_top):
    middle_charge = restrict(charge)
    top_charge = restrict(middle_charge)
    top_potential = convolve(top_charge, kernel_top)
    middle_potential = convolve(middle_charge, kernel_mid) + prolong(top_potential)
    return convolve(charge, kernel_fine) + prolong(middle_potential)
```

```python
import functools

import jax
import jax.numpy as jnp
from jax import lax
from jax.experimental import pallas as pl
from jax.experimental.pallas import tpu as pltpu
from jax.sharding import PartitionSpec as P

BF = jnp.bfloat16
F32 = jnp.float32
SPLINE = (0.125, 0.5, 0.75, 0.5, 0.125)
EDGE, MIDDLE, HALF = 0.125, 0.75, 0.5
TAPS = 11
RADIUS = 5

FX, FROW = 5, 8
MX, TX = 6, 6


def messages():
    fine, middle, top = [], [], []
    for dx in (-1, 0, 1):
        sx = {1: (43, 5), 0: (0, 48), -1: (0, 5)}[dx]
        tx = {1: 0, 0: 5, -1: 53}[dx]
        for dy in (-1, 0, 1):
            if dx == 0 and dy == 0:
                continue
            sy = {1: (3, 5), 0: (0, 8), -1: (0, 5)}[dy]
            ty = {1: 3, 0: 8, -1: 16}[dy]
            fine.append((dx, dy, sx, sy, tx, ty))
    for dx in (0, -1, 1):
        sx = {1: (24, 6), 0: (6, 24), -1: (6, 6)}[dx]
        tx = {1: 0, 0: 6, -1: 30}[dx]
        for dy in (-2, -1, 0, 1, 2):
            if dx == 0 and dy == 0:
                continue
            sy = {2: (10, 2), 1: (8, 4), 0: (8, 4), -1: (8, 4), -2: (8, 2)}[dy]
            ty = {2: 2, 1: 4, 0: 8, -1: 12, -2: 16}[dy]
            middle.append((dx, dy, sx, sy, tx, ty))
    for dx in (0, -1, 1):
        sx = {1: (12, 6), 0: (6, 12), -1: (6, 7)}[dx]
        tx = {1: 0, 0: 6, -1: 18}[dx]
        for dy in (-4, -3, -2, -1, 0, 1, 2, 3):
            if dx == 0 and dy == 0:
                continue
            top.append((dx, dy, sx, (8, 2), tx, 8 - 2 * dy))
    return fine, middle, top


FINE, MIDDLE_MSG, TOP = messages()
COUNT = len(FINE) + len(MIDDLE_MSG) + len(TOP)
REACH = 4


def split(value):
    high = value.astype(BF)
    return high, (value - high.astype(F32)).astype(BF)


def dot(a, b):
    return jnp.dot(a, b, preferred_element_type=F32)


def exact_dot(value, weights):
    high, low = split(value)
    return dot(high, weights) + dot(low, weights)


def base_rows(kernel_ref, padded, rows, z):
    per = 128 // z
    padded[...] = jnp.zeros_like(padded)
    padded[0:TAPS, 0:TAPS, 0:TAPS] = kernel_ref[...]
    tap = lax.broadcasted_iota(jnp.int32, (128, per * 128), 0)
    lane = lax.broadcasted_iota(jnp.int32, (128, per * 128), 1)
    place = (lane // 128) * z + RADIUS - tap
    spread = ((lane - place) % 128 == 0) & (tap < TAPS)
    spread = spread.astype(F32).astype(BF)
    table = exact_dot(padded[...].reshape(256, 128), spread).reshape(16, 16, per * 128)
    for n in range(rows.shape[0]):
        total = None
        for q in range(per):
            piece = table[n * per + q, :, q * 128 : (q + 1) * 128]
            total = piece if total is None else total + piece
        rows[n] = total


def toeplitz(rows, high_ref, low_ref, z, depth):
    groups = rows.shape[0] // 2
    lane = lax.broadcasted_iota(jnp.int32, (16, 128), 1) % z
    early, late = lane < z - 8, lane >= 8

    def group(i, _):
        for half in range(2):
            for b in range(TAPS):
                row = jnp.broadcast_to(rows[2 * i + half, b : b + 1, :], (16, 128))
                tile = pltpu.roll(row, 0, 1, stride=1, stride_axis=0)
                for t in range(z // 16):
                    part = pltpu.roll(tile, 16 * t, 1) if t else tile
                    if t == 0:
                        part = jnp.where(early, part, 0.0)
                    if t == z // 16 - 1:
                        part = jnp.where(late, part, 0.0)
                    high, low = split(part)
                    start = pl.multiple_of(i * depth + b * z + 16 * t, 16)
                    high_ref[pl.ds(start, 16), half * 128 : half * 128 + 128] = high
                    low_ref[pl.ds(start, 16), half * 128 : half * 128 + 128] = low
        if depth > TAPS * z:
            start = pl.multiple_of(i * depth + TAPS * z, 16)
            for ref in (high_ref, low_ref):
                ref[pl.ds(start, depth - TAPS * z), :] = jnp.zeros((depth - TAPS * z, 256), BF)
        return 0

    lax.fori_loop(0, groups, group, 0)


def gather_taps(window, high_ref, low_ref, first_row, z):
    per = 128 // z

    def pair(p, _):
        for lane_block in range(high_ref.shape[2] // 128):
            pieces = []
            for q in range(per):
                row = first_row + lane_block * per + q
                pieces.append(window[pl.ds(2 * p, 2), row : row + 8, :])
            value = pieces[0] if per == 1 else jnp.concatenate(pieces, axis=-1)
            high, low = split(value.reshape(16, 128))
            at = slice(lane_block * 128, lane_block * 128 + 128)
            high_ref[p, :, at] = high
            low_ref[p, :, at] = low
        return 0

    lax.fori_loop(0, high_ref.shape[0], pair, 0)


def products(ah, al, wh, wl):
    return dot(ah, wh) + dot(al, wh) + dot(ah, wl)


def small_convolution(high_a, low_a, high_w, low_w, pairs, step, groups, depth, z, planes):
    total = None
    for i in range(groups):
        ah = high_a[i * step : i * step + pairs].reshape(pairs * 16, depth)
        al = low_a[i * step : i * step + pairs].reshape(pairs * 16, depth)
        at = slice(i * depth, (i + 1) * depth)
        part = products(ah, al, high_w[at], low_w[at])
        total = part if total is None else total + part
    total = total.reshape(pairs * 2, 8, 256)
    result = None
    for j in range(256 // z):
        piece = total[j : j + planes, :, j * z : (j + 1) * z]
        result = piece if result is None else result + piece
    return result


def fine_step(i, high_a, low_a, high_w, low_w, total):
    def rows(ref):
        first = ref[pl.ds(2 * i, 25)].reshape(400, 1408)
        second = ref[pl.ds(2 * i + 1, 25)].reshape(400, 1408)
        return jnp.concatenate([first, second], axis=-1)

    at = pl.ds(pl.multiple_of(i * 2816, 2816), 2816)
    total[...] += products(rows(high_a), rows(low_a), high_w[at], low_w[at])


def restrict_matrix(z):
    source = lax.broadcasted_iota(jnp.int32, (z, z // 2), 0)
    target = lax.broadcasted_iota(jnp.int32, (z, z // 2), 1)
    away = jnp.abs(source - 2 * target)
    weight = jnp.where(away == 0, 0.75, jnp.where(away == 1, 0.5, jnp.where(away == 2, 0.125, 0.0)))
    return weight.astype(F32).astype(BF)


def prolong_matrix(z):
    source = lax.broadcasted_iota(jnp.int32, (z, 2 * z), 0)
    target = lax.broadcasted_iota(jnp.int32, (z, 2 * z), 1)
    away = jnp.abs(target - 2 * source)
    weight = jnp.where(away == 0, 0.75, jnp.where(away == 1, 0.5, jnp.where(away == 2, 0.125, 0.0)))
    return weight.astype(F32).astype(BF)


def restrict(window, along_x, first_plane, first_row, planes, z):
    for i in range(planes):
        total = None
        for a, weight in enumerate(SPLINE):
            piece = weight * window[first_plane + 2 * i + a - 2]
            total = piece if total is None else total + piece
        along_x[i, 0:24, :] = total
    rows = None
    for b, weight in enumerate(SPLINE):
        piece = weight * along_x[:, pl.ds(first_row + b - 2, 8, stride=2), :]
        rows = piece if rows is None else rows + piece
    result = exact_dot(rows.reshape(planes * 8, z), restrict_matrix(z))
    return result.reshape(planes, 8, z // 2)


def inside(planes, first_x, count_x, first_y, count_y, z):
    x = first_x + lax.broadcasted_iota(jnp.int32, (planes, 8, z), 0)
    y = first_y + lax.broadcasted_iota(jnp.int32, (planes, 8, z), 1)
    return (x >= 0) & (x < count_x) & (y >= 0) & (y < count_y)


def whole(
    nx, ny,
    charge, kernel_fine, kernel_mid, kernel_top, out,
    fine, along_fine, middle, along_middle, top, padded, rows_f, rows_m, rows_t,
    wfh, wfl, wmh, wml, wth, wtl, afh, afl, amh, aml, ath, atl,
    total, pot_z, pot_y, top_z, top_y, send_sems, recv_sems,
):
    gx, gy = lax.axis_index("gx"), lax.axis_index("gy")

    def exists(dx, dy):
        return (gx + dx >= 0) & (gx + dx < nx) & (gy + dy >= 0) & (gy + dy < ny)

    def transfer(number, message, source, target):
        dx, dy, (px, lx), (py, ly), tx, ty = message
        return pltpu.make_async_remote_copy(
            src_ref=source.at[pl.ds(px, lx), pl.ds(py, ly)],
            dst_ref=target.at[pl.ds(tx, lx), pl.ds(ty, ly)],
            send_sem=send_sems.at[number],
            recv_sem=recv_sems.at[number],
            device_id={"gx": gx + dx, "gy": gy + dy},
            device_id_type=pl.DeviceIdType.MESH,
        )

    def start(first, group, source, target):
        for k, message in enumerate(group):
            @pl.when(exists(message[0], message[1]))
            def _(k=k, message=message):
                transfer(first + k, message, source, target).start()

    def arrive(first, group, source, target):
        for k, message in enumerate(group):
            @pl.when(exists(-message[0], -message[1]))
            def _(k=k, message=message):
                transfer(first + k, message, source, target).wait_recv()

    def sent(first, group, source, target):
        for k, message in enumerate(group):
            @pl.when(exists(message[0], message[1]))
            def _(k=k, message=message):
                transfer(first + k, message, source, target).wait_send()

    n_fine, n_middle = len(FINE), len(FINE) + len(MIDDLE_MSG)

    fine[...] = jnp.zeros_like(fine)
    fine[FX : FX + 48, FROW : FROW + 8, :] = charge[...]
    middle[...] = jnp.zeros_like(middle)
    top[...] = jnp.zeros_like(top)
    along_fine[...] = jnp.zeros_like(along_fine)
    along_middle[...] = jnp.zeros_like(along_middle)

    barrier = pltpu.get_barrier_semaphore()
    for dx in (-1, 0, 1):
        for dy in range(-REACH, REACH + 1):
            if dx == 0 and dy == 0:
                continue
            @pl.when(exists(dx, dy))
            def _(dx=dx, dy=dy):
                pl.semaphore_signal(
                    barrier, inc=1, device_id={"gx": gx + dx, "gy": gy + dy},
                    device_id_type=pl.DeviceIdType.MESH,
                )

    base_rows(kernel_mid, padded, rows_m, 64)
    toeplitz(rows_m, wmh, wml, 64, 768)
    base_rows(kernel_top, padded, rows_t, 32)
    toeplitz(rows_t, wth, wtl, 32, 384)
    base_rows(kernel_fine, padded, rows_f, 128)

    across = 1 + (gx > 0).astype(jnp.int32) + (gx < nx - 1).astype(jnp.int32)
    along = 1 + jnp.minimum(gy, REACH) + jnp.minimum(ny - 1 - gy, REACH)
    pl.semaphore_wait(barrier, across * along - 1)

    start(0, FINE, charge, fine)
    toeplitz(rows_f, wfh, wfl, 128, 1408)
    arrive(0, FINE, charge, fine)

    middle_block = restrict(fine, along_fine, FX, FROW, 24, 128)
    middle[MX : MX + 24, 8:12, :] = middle_block[:, 0:4, :]
    start(n_fine, MIDDLE_MSG, middle, middle)

    gather_taps(fine, afh, afl, 3, 128)
    total[...] = jnp.zeros_like(total)
    fine_step(0, afh, afl, wfh, wfl, total)

    arrive(n_fine, MIDDLE_MSG, middle, middle)
    top_block = restrict(middle, along_middle, MX, 8, 12, 64)
    top[TX : TX + 12, 8:10, :] = top_block[:, 0:2, :]
    start(n_middle, TOP, top, top)

    def step(i, _):
        fine_step(i, afh, afl, wfh, wfl, total)
        return 0

    lax.fori_loop(1, 3, step, 0)
    gather_taps(middle, amh, aml, 2, 64)

    arrive(n_middle, TOP, top, top)
    gather_taps(top, ath, atl, 2, 32)
    top_pot = small_convolution(ath, atl, wth, wtl, 11, 4, 2, 384, 32, 15)
    top_pot = jnp.where(inside(15, gx * 12 - 1, nx * 12, gy * 2 - 1, ny * 2, 32), top_pot, 0.0)
    top_z[...] = exact_dot(top_pot.reshape(120, 32), prolong_matrix(32)).reshape(15, 8, 64)
    e0, e1, e2 = top_z[:, 0:3, :], top_z[:, 1:4, :], top_z[:, 2:5, :]
    top_y[...] = jnp.zeros_like(top_y)
    top_y[:, pl.ds(0, 3, stride=2), :] = HALF * e0 + HALF * e1
    top_y[:, pl.ds(1, 3, stride=2), :] = EDGE * e0 + MIDDLE * e1 + EDGE * e2

    mid_pot = small_convolution(amh, aml, wmh, wml, 15, 2, 3, 768, 64, 26)
    pieces = []
    for k in range(13):
        f0, f1, f2 = top_y[k], top_y[k + 1], top_y[k + 2]
        pieces.append((HALF * f0 + HALF * f1)[None])
        pieces.append((EDGE * f0 + MIDDLE * f1 + EDGE * f2)[None])
    mid_pot = mid_pot + jnp.concatenate(pieces, axis=0)
    mid_pot = jnp.where(inside(26, gx * 24 - 1, nx * 24, gy * 4 - 1, ny * 4, 64), mid_pot, 0.0)
    pot_z[...] = exact_dot(mid_pot.reshape(208, 64), prolong_matrix(64)).reshape(26, 8, 128)
    e0, e1, e2 = pot_z[:, 0:4, :], pot_z[:, 1:5, :], pot_z[:, 2:6, :]
    pot_y[:, pl.ds(0, 4, stride=2), :] = EDGE * e0 + MIDDLE * e1 + EDGE * e2
    pot_y[:, pl.ds(1, 4, stride=2), :] = HALF * e1 + HALF * e2

    for m in range(24):
        f0, f1, f2 = pot_y[m], pot_y[m + 1], pot_y[m + 2]
        for odd in range(2):
            x = 2 * m + odd
            near = total[8 * x : 8 * x + 8, 0:128]
            far = total[8 * x + 8 : 8 * x + 16, 128:256]
            fill = HALF * f1 + HALF * f2 if odd else EDGE * f0 + MIDDLE * f1 + EDGE * f2
            out[x] = near + far + fill

    sent(0, FINE, charge, fine)
    sent(n_fine, MIDDLE_MSG, middle, middle)
    sent(n_middle, TOP, top, top)


def solution(mesh):
    nx, ny = mesh.shape["gx"], mesh.shape["gy"]
    vmem = pltpu.VMEM
    scratch = [
        vmem((60, 24, 128), F32), vmem((24, 32, 128), F32), vmem((40, 24, 64), F32),
        vmem((12, 32, 64), F32), vmem((32, 24, 32), F32), vmem((16, 16, 128), F32),
        vmem((12, 16, 128), F32), vmem((6, 16, 128), F32), vmem((4, 16, 128), F32),
        vmem((8448, 256), BF), vmem((8448, 256), BF), vmem((2304, 256), BF), vmem((2304, 256), BF),
        vmem((768, 256), BF), vmem((768, 256), BF),
        vmem((30, 16, 1408), BF), vmem((30, 16, 1408), BF), vmem((19, 16, 768), BF),
        vmem((19, 16, 768), BF), vmem((15, 16, 384), BF), vmem((15, 16, 384), BF),
        vmem((400, 256), F32), vmem((26, 8, 128), F32), vmem((26, 8, 128), F32),
        vmem((15, 8, 64), F32), vmem((15, 8, 64), F32),
        pltpu.SemaphoreType.DMA((COUNT,)), pltpu.SemaphoreType.DMA((COUNT,)),
    ]

    def shards(charge, kernel_fine, kernel_mid, kernel_top):
        return pl.pallas_call(
            functools.partial(whole, nx, ny),
            out_shape=jax.ShapeDtypeStruct(charge.shape, F32),
            in_specs=[pl.BlockSpec(memory_space=pltpu.VMEM)] * 4,
            out_specs=pl.BlockSpec(memory_space=pltpu.VMEM),
            scratch_shapes=scratch,
            compiler_params=pltpu.CompilerParams(
                collective_id=0, has_side_effects=True, vmem_limit_bytes=60 << 20
            ),
            name="multilevel",
        )(charge, kernel_fine, kernel_mid, kernel_top)

    return jax.shard_map(
        shards, mesh=mesh, in_specs=(P("gx", "gy", None), P(), P(), P()),
        out_specs=P("gx", "gy", None), check_vma=False,
    )
```

```python
import functools

import jax
import jax.numpy as jnp
from jax import lax
from jax.experimental import pallas as pl
from jax.experimental.pallas import tpu as pltpu
from jax.sharding import PartitionSpec as P

BF = jnp.bfloat16
F32 = jnp.float32
SPLINE = (0.125, 0.5, 0.75, 0.5, 0.125)
EDGE, MIDDLE, HALF = 0.125, 0.75, 0.5
TAPS = 11
RADIUS = 5

FX, FROW = 6, 8
MX, TX = 6, 6
REACH = 4


def messages():
    fine, middle, top = [], [], []
    for dx in (-1, 0, 1):
        sx = {1: (42, 6), 0: (0, 48), -1: (0, 5)}[dx]
        tx = {1: 0, 0: 6, -1: 54}[dx]
        for dy in (-1, 0, 1):
            sy = {1: (2, 6), 0: (0, 8), -1: (0, 5)}[dy]
            ty = {1: 2, 0: 8, -1: 16}[dy]
            fine.append((dx, dy, sx, sy, tx, ty))
        sx = {1: (24, 6), 0: (6, 24), -1: (6, 6)}[dx]
        tx = {1: 0, 0: 6, -1: 30}[dx]
        for dy in range(-2, 3):
            sy = {2: (10, 2), -2: (8, 2)}.get(dy, (8, 4))
            ty = {2: 2, 1: 4, 0: 8, -1: 12, -2: 16}[dy]
            middle.append((dx, dy, sx, sy, tx, ty))
        sx = {1: (12, 6), 0: (6, 12), -1: (6, 7)}[dx]
        tx = {1: 0, 0: 6, -1: 18}[dx]
        for dy in range(-4, 4):
            top.append((dx, dy, sx, (8, 2), tx, 8 - 2 * dy))
    return [[m for m in group if m[:2] != (0, 0)] for group in (fine, middle, top)]


FINE, MIDDLE_MSG, TOP = messages()
EVERY = FINE + MIDDLE_MSG + TOP
COUNT = len(EVERY)
N_FINE = len(FINE)
N_MIDDLE = N_FINE + len(MIDDLE_MSG)


def split(value):
    high = value.astype(BF)
    return high, (value - high.astype(F32)).astype(BF)


def dot(a, b):
    return jnp.dot(a, b, preferred_element_type=F32)


def exact_dot(value, weights):
    high, low = split(value)
    return dot(high, weights) + dot(low, weights)


def base_rows(kernel_ref, padded, rows, z):
    per = 128 // z
    padded[...] = jnp.zeros_like(padded)
    padded[0:TAPS, 0:TAPS, 0:TAPS] = kernel_ref[...]
    tap = lax.broadcasted_iota(jnp.int32, (128, per * 128), 0)
    lane = lax.broadcasted_iota(jnp.int32, (128, per * 128), 1)
    place = (lane // 128) * z + RADIUS - tap
    spread = ((lane - place) % 128 == 0) & (tap < TAPS)
    spread = spread.astype(F32).astype(BF)
    table = exact_dot(padded[...].reshape(256, 128), spread).reshape(16, 16, per * 128)
    for n in range(rows.shape[0]):
        total = None
        for q in range(per):
            piece = table[n * per + q, :, q * 128 : (q + 1) * 128]
            total = piece if total is None else total + piece
        rows[n] = total


def shift_matrix(z, first, tiles):
    source = lax.broadcasted_iota(jnp.int32, (128, tiles * 128), 0)
    target = lax.broadcasted_iota(jnp.int32, (128, tiles * 128), 1)
    ahead = 16 * (target // 128 + first)
    cell = target % z
    keep = ((source + ahead - target) % 128 == 0) & (cell >= ahead - RADIUS) & (cell <= ahead + 20)
    return keep.astype(F32).astype(BF)


def toeplitz(rows, high_ref, low_ref, z, depth, rolled):
    groups, tiles = rows.shape[0] // 2, z // 16
    shifts = shift_matrix(z, rolled, tiles - rolled)
    early = lax.broadcasted_iota(jnp.int32, (16, 128), 1) % z < z - 8

    def group(i, _):
        for half in range(2):
            at = slice(half * 128, half * 128 + 128)

            def place(ref, b, t, tile):
                ref[pl.ds(pl.multiple_of(i * depth + b * z + 16 * t, 16), 16), at] = tile

            firsts = []
            for b in range(TAPS):
                row = jnp.broadcast_to(rows[2 * i + half, b : b + 1, :], (16, 128))
                firsts.append(pltpu.roll(row, 0, 1, stride=1, stride_axis=0))
            for part, ref in zip(split(jnp.concatenate(firsts, axis=0)), (high_ref, low_ref)):
                moved = dot(part, shifts).astype(BF)
                for b in range(TAPS):
                    for t in range(rolled, tiles):
                        lanes = slice(128 * (t - rolled), 128 * (t - rolled) + 128)
                        place(ref, b, t, moved[16 * b : 16 * b + 16, lanes])
            for b in range(TAPS):
                for t in range(rolled):
                    tile = pltpu.roll(firsts[b], 16 * t, 1) if t else jnp.where(early, firsts[b], 0.0)
                    for part, ref in zip(split(tile), (high_ref, low_ref)):
                        place(ref, b, t, part)
        if depth > TAPS * z:
            start = pl.multiple_of(i * depth + TAPS * z, 16)
            for ref in (high_ref, low_ref):
                ref[pl.ds(start, depth - TAPS * z), :] = jnp.zeros((depth - TAPS * z, 256), BF)
        return 0

    lax.fori_loop(0, groups, group, 0)


def gather_taps(window, high_ref, low_ref, first_plane, first_row, z):
    per = 128 // z

    def pair(p, _):
        for lane_block in range(high_ref.shape[2] // 128):
            pieces = []
            for q in range(per):
                row = first_row + lane_block * per + q
                pieces.append(window[pl.ds(first_plane + 2 * p, 2), row : row + 8, :])
            value = pieces[0] if per == 1 else jnp.concatenate(pieces, axis=-1)
            high, low = split(value.reshape(16, 128))
            at = slice(lane_block * 128, lane_block * 128 + 128)
            high_ref[p, :, at] = high
            low_ref[p, :, at] = low
        return 0

    lax.fori_loop(0, high_ref.shape[0], pair, 0)


def products(ah, al, wh, wl):
    return dot(ah, wh) + dot(al, wh) + dot(ah, wl)


def small_convolution(high_a, low_a, high_w, low_w, pairs, step, groups, depth, z, planes):
    total = None
    for i in range(groups):
        ah = high_a[i * step : i * step + pairs].reshape(pairs * 16, depth)
        al = low_a[i * step : i * step + pairs].reshape(pairs * 16, depth)
        at = slice(i * depth, (i + 1) * depth)
        part = products(ah, al, high_w[at], low_w[at])
        total = part if total is None else total + part
    total = total.reshape(pairs * 2, 8, 256)
    result = None
    for j in range(256 // z):
        piece = total[j : j + planes, :, j * z : (j + 1) * z]
        result = piece if result is None else result + piece
    return result


def fine_step(i, high_a, low_a, high_w, low_w, total):
    def rows(ref):
        first = ref[pl.ds(2 * i, 25)].reshape(400, 1408)
        second = ref[pl.ds(2 * i + 1, 25)].reshape(400, 1408)
        return jnp.concatenate([first, second], axis=-1)

    at = pl.ds(i * 2816, 2816)
    total[...] += products(rows(high_a), rows(low_a), high_w[at], low_w[at])


def restrict_matrix(z):
    source = lax.broadcasted_iota(jnp.int32, (z, z // 2), 0)
    target = lax.broadcasted_iota(jnp.int32, (z, z // 2), 1)
    away = jnp.abs(source - 2 * target)
    weight = jnp.where(away == 0, 0.75, jnp.where(away == 1, 0.5, jnp.where(away == 2, 0.125, 0.0)))
    return weight.astype(F32).astype(BF)


def prolong_matrix(z):
    source = lax.broadcasted_iota(jnp.int32, (z, 2 * z), 0)
    target = lax.broadcasted_iota(jnp.int32, (z, 2 * z), 1)
    away = jnp.abs(target - 2 * source)
    weight = jnp.where(away == 0, 0.75, jnp.where(away == 1, 0.5, jnp.where(away == 2, 0.125, 0.0)))
    return weight.astype(F32).astype(BF)


def restrict(block, along_x, first_plane, first_row, at, z):
    planes = along_x.shape[0]
    for i in range(planes):
        total = None
        for a, weight in enumerate(SPLINE):
            source = first_plane + 2 * i + a
            if 0 <= source < block.shape[0]:
                piece = weight * block[source]
                total = piece if total is None else total + piece
        along_x[i, at : at + block.shape[1], :] = total
    rows = None
    for b, weight in enumerate(SPLINE):
        piece = weight * along_x[:, pl.ds(first_row + b, 8, stride=2), :]
        rows = piece if rows is None else rows + piece
    result = exact_dot(rows.reshape(planes * 8, z), restrict_matrix(z))
    return result.reshape(planes, 8, z // 2)


def inside(planes, first_x, count_x, first_y, count_y, z):
    x = first_x + lax.broadcasted_iota(jnp.int32, (planes, 8, z), 0)
    y = first_y + lax.broadcasted_iota(jnp.int32, (planes, 8, z), 1)
    return (x >= 0) & (x < count_x) & (y >= 0) & (y < count_y)


def whole(
    nx, ny,
    charge_hbm, kernel_fine_hbm, kernel_mid_hbm, kernel_top_hbm, out,
    charge, kernel_fine, kernel_mid, kernel_top,
    fine, along_fine, middle, along_middle, top,
    padded, rows_f, rows_m, rows_t,
    wfh, wfl, wmh, wml, wth, wtl, afh, afl, amh, aml, ath, atl,
    total, pot_z, pot_y, top_z, top_y, load_sems, send_sems, recv_sems,
):
    gx, gy = lax.axis_index("gx"), lax.axis_index("gy")

    loads = [
        pltpu.make_async_copy(source, target, load_sems.at[n])
        for n, (source, target) in enumerate((
            (charge_hbm, charge), (kernel_mid_hbm, kernel_mid),
            (kernel_top_hbm, kernel_top), (kernel_fine_hbm, kernel_fine),
        ))
    ]
    for load in loads:
        load.start()

    def exists(dx, dy):
        return (gx + dx >= 0) & (gx + dx < nx) & (gy + dy >= 0) & (gy + dy < ny)

    def transfer(number):
        dx, dy, (px, lx), (py, ly), tx, ty = EVERY[number]
        if number < N_FINE:
            source, target = charge, fine.at[pl.ds(tx, lx), pl.ds(ty, ly)]
        else:
            source = middle if number < N_MIDDLE else top
            target = source.at[pl.ds(tx, lx), pl.ds(ty, ly)]
        return pltpu.make_async_remote_copy(
            src_ref=source.at[pl.ds(px, lx), pl.ds(py, ly)], dst_ref=target,
            send_sem=send_sems.at[number], recv_sem=recv_sems.at[number],
            device_id={"gx": gx + dx, "gy": gy + dy},
            device_id_type=pl.DeviceIdType.MESH,
        )

    def start(numbers):
        for number in numbers:
            @pl.when(exists(EVERY[number][0], EVERY[number][1]))
            def _(number=number):
                transfer(number).start()

    def arrive(numbers):
        for number in numbers:
            @pl.when(exists(-EVERY[number][0], -EVERY[number][1]))
            def _(number=number):
                transfer(number).wait_recv()

    def sent(numbers):
        for number in numbers:
            @pl.when(exists(EVERY[number][0], EVERY[number][1]))
            def _(number=number):
                transfer(number).wait_send()

    for ref in (fine, middle, top):
        ref[...] = jnp.zeros_like(ref)

    barrier = pltpu.get_barrier_semaphore()
    for dx in (-1, 0, 1):
        for dy in range(-REACH, REACH + 1):
            if dx == 0 and dy == 0:
                continue
            @pl.when(exists(dx, dy))
            def _(dx=dx, dy=dy):
                pl.semaphore_signal(
                    barrier, inc=1, device_id={"gx": gx + dx, "gy": gy + dy},
                    device_id_type=pl.DeviceIdType.MESH,
                )

    for ref in (along_fine, along_middle):
        ref[...] = jnp.zeros_like(ref)
    for load in loads:
        load.wait()

    fine[FX : FX + 48, FROW : FROW + 8, :] = charge[...]
    base_rows(kernel_mid, padded, rows_m, 64)
    toeplitz(rows_m, wmh, wml, 64, 768, 2)
    base_rows(kernel_top, padded, rows_t, 32)
    toeplitz(rows_t, wth, wtl, 32, 384, 1)
    base_rows(kernel_fine, padded, rows_f, 128)

    across = 1 + (gx > 0).astype(jnp.int32) + (gx < nx - 1).astype(jnp.int32)
    along = 1 + jnp.minimum(gy, REACH) + jnp.minimum(ny - 1 - gy, REACH)
    pl.semaphore_wait(barrier, across * along - 1)

    start(range(N_FINE))
    toeplitz(rows_f, wfh, wfl, 128, 1408, 5)
    arrive(range(N_FINE))

    near = restrict(fine, along_fine, 0, 2, 0, 128)
    near = jnp.where(inside(27, gx * 24 - 2, nx * 24, gy * 4 - 2, ny * 4, 64), near, 0.0)
    middle[MX : MX + 24, 8:12, :] = near[2:26, 2:6, :]
    top[TX : TX + 12, 8:10, :] = restrict(near, along_middle, 0, 8, 8, 64)[:, 0:2, :]
    start(range(N_FINE, COUNT))

    gather_taps(fine, afh, afl, 1, 3, 128)
    total[...] = jnp.zeros_like(total)

    for i in range(3):
        fine_step(i, afh, afl, wfh, wfl, total)

    arrive(range(N_FINE, N_MIDDLE))
    gather_taps(middle, amh, aml, 0, 2, 64)
    arrive(range(N_MIDDLE, COUNT))
    gather_taps(top, ath, atl, 0, 2, 32)
    top_pot = small_convolution(ath, atl, wth, wtl, 11, 4, 2, 384, 32, 15)
    top_pot = jnp.where(inside(15, gx * 12 - 1, nx * 12, gy * 2 - 1, ny * 2, 32), top_pot, 0.0)
    top_z[...] = exact_dot(top_pot.reshape(120, 32), prolong_matrix(32)).reshape(15, 8, 64)
    e0, e1, e2 = top_z[:, 0:3, :], top_z[:, 1:4, :], top_z[:, 2:5, :]
    top_y[...] = jnp.zeros_like(top_y)
    top_y[:, pl.ds(0, 3, stride=2), :] = HALF * e0 + HALF * e1
    top_y[:, pl.ds(1, 3, stride=2), :] = EDGE * e0 + MIDDLE * e1 + EDGE * e2

    mid_pot = small_convolution(amh, aml, wmh, wml, 15, 2, 3, 768, 64, 26)
    pieces = []
    for k in range(13):
        f0, f1, f2 = top_y[k], top_y[k + 1], top_y[k + 2]
        pieces.append((HALF * f0 + HALF * f1)[None])
        pieces.append((EDGE * f0 + MIDDLE * f1 + EDGE * f2)[None])
    mid_pot = mid_pot + jnp.concatenate(pieces, axis=0)
    mid_pot = jnp.where(inside(26, gx * 24 - 1, nx * 24, gy * 4 - 1, ny * 4, 64), mid_pot, 0.0)
    pot_z[...] = exact_dot(mid_pot.reshape(208, 64), prolong_matrix(64)).reshape(26, 8, 128)
    e0, e1, e2 = pot_z[:, 0:4, :], pot_z[:, 1:5, :], pot_z[:, 2:6, :]
    pot_y[:, pl.ds(0, 4, stride=2), :] = EDGE * e0 + MIDDLE * e1 + EDGE * e2
    pot_y[:, pl.ds(1, 4, stride=2), :] = HALF * e1 + HALF * e2

    for m in range(24):
        f0, f1, f2 = pot_y[m], pot_y[m + 1], pot_y[m + 2]
        for odd in range(2):
            x = 2 * m + odd
            near = total[8 * x : 8 * x + 8, 0:128]
            far = total[8 * x + 8 : 8 * x + 16, 128:256]
            fill = HALF * f1 + HALF * f2 if odd else EDGE * f0 + MIDDLE * f1 + EDGE * f2
            out[x] = near + far + fill

    sent(range(COUNT))


def solution(mesh):
    nx, ny = mesh.shape["gx"], mesh.shape["gy"]
    vmem = pltpu.VMEM
    scratch = [
        vmem((48, 8, 128), F32), vmem((11, 11, 11), F32), vmem((11, 11, 11), F32),
        vmem((11, 11, 11), F32),
        vmem((62, 24, 128), F32), vmem((27, 32, 128), F32), vmem((40, 24, 64), F32),
        vmem((12, 32, 64), F32), vmem((32, 24, 32), F32), vmem((16, 16, 128), F32),
        vmem((12, 16, 128), F32), vmem((6, 16, 128), F32), vmem((4, 16, 128), F32),
        vmem((8448, 256), BF), vmem((8448, 256), BF), vmem((2304, 256), BF), vmem((2304, 256), BF),
        vmem((768, 256), BF), vmem((768, 256), BF),
        vmem((30, 16, 1408), BF), vmem((30, 16, 1408), BF), vmem((19, 16, 768), BF),
        vmem((19, 16, 768), BF), vmem((15, 16, 384), BF), vmem((15, 16, 384), BF),
        vmem((400, 256), F32), vmem((26, 8, 128), F32), vmem((26, 8, 128), F32),
        vmem((15, 8, 64), F32), vmem((15, 8, 64), F32),
        pltpu.SemaphoreType.DMA((4,)),
        pltpu.SemaphoreType.DMA((COUNT,)), pltpu.SemaphoreType.DMA((COUNT,)),
    ]

    def shards(charge, kernel_fine, kernel_mid, kernel_top):
        return pl.pallas_call(
            functools.partial(whole, nx, ny),
            out_shape=jax.ShapeDtypeStruct(charge.shape, F32),
            in_specs=[pl.BlockSpec(memory_space=pl.ANY)] * 4,
            out_specs=pl.BlockSpec(memory_space=pltpu.VMEM),
            scratch_shapes=scratch,
            compiler_params=pltpu.CompilerParams(
                collective_id=0, has_side_effects=True, vmem_limit_bytes=60 << 20
            ),
            name="multilevel",
        )(charge, kernel_fine, kernel_mid, kernel_top)

    return jax.shard_map(
        shards, mesh=mesh, in_specs=(P("gx", "gy", None), P(), P(), P()),
        out_specs=P("gx", "gy", None), check_vma=False,
    )
```

```python
import functools

import jax
import jax.numpy as jnp
from jax import lax
from jax.experimental import pallas as pl
from jax.experimental.pallas import tpu as pltpu
from jax.sharding import PartitionSpec as P

BF = jnp.bfloat16
F32 = jnp.float32
SPLINE = (0.125, 0.5, 0.75, 0.5, 0.125)
EDGE, MIDDLE, HALF = 0.125, 0.75, 0.5
TAPS = 11
RADIUS = 5

FX, FROW = 6, 8
MX, TX = 6, 6
REACH = 4


def messages():
    fine, middle, top = [], [], []
    for dx in (-1, 0, 1):
        sx = {1: (42, 6), 0: (0, 48), -1: (0, 5)}[dx]
        tx = {1: 0, 0: 6, -1: 54}[dx]
        for dy in (-1, 0, 1):
            sy = {1: (2, 6), 0: (0, 8), -1: (0, 5)}[dy]
            ty = {1: 2, 0: 8, -1: 16}[dy]
            fine.append((dx, dy, sx, sy, tx, ty))
        sx = {1: (24, 6), 0: (6, 24), -1: (6, 6)}[dx]
        tx = {1: 0, 0: 6, -1: 30}[dx]
        for dy in range(-2, 3):
            sy = {2: (10, 2), -2: (8, 2)}.get(dy, (8, 4))
            ty = {2: 2, 1: 4, 0: 8, -1: 12, -2: 16}[dy]
            middle.append((dx, dy, sx, sy, tx, ty))
        sx = {1: (12, 6), 0: (6, 12), -1: (6, 7)}[dx]
        tx = {1: 0, 0: 6, -1: 18}[dx]
        for dy in range(-4, 4):
            top.append((dx, dy, sx, (8, 2), tx, 8 - 2 * dy))
    return [[m for m in group if m[:2] != (0, 0)] for group in (fine, middle, top)]


FINE, MIDDLE_MSG, TOP = messages()
EVERY = FINE + MIDDLE_MSG + TOP
COUNT = len(EVERY)
N_FINE = len(FINE)
N_MIDDLE = N_FINE + len(MIDDLE_MSG)


def split(value):
    high = value.astype(BF)
    return high, (value - high.astype(F32)).astype(BF)


def dot(a, b):
    return jnp.dot(a, b, preferred_element_type=F32)


def exact_dot(value, weights):
    high, low = split(value)
    return dot(high, weights) + dot(low, weights)


def base_rows(kernel_ref, padded, rows, z):
    per = 128 // z
    padded[...] = jnp.zeros_like(padded)
    padded[0:TAPS, 0:TAPS, 0:TAPS] = kernel_ref[...]
    tap = lax.broadcasted_iota(jnp.int32, (128, per * 128), 0)
    lane = lax.broadcasted_iota(jnp.int32, (128, per * 128), 1)
    place = (lane // 128) * z + RADIUS - tap
    spread = ((lane - place) % 128 == 0) & (tap < TAPS)
    spread = spread.astype(F32).astype(BF)
    table = exact_dot(padded[...].reshape(256, 128), spread).reshape(16, 16, per * 128)
    for n in range(rows.shape[0]):
        total = None
        for q in range(per):
            piece = table[n * per + q, :, q * 128 : (q + 1) * 128]
            total = piece if total is None else total + piece
        rows[n] = total


def shift_matrix(z, first, tiles):
    source = lax.broadcasted_iota(jnp.int32, (128, tiles * 128), 0)
    target = lax.broadcasted_iota(jnp.int32, (128, tiles * 128), 1)
    ahead = 16 * (target // 128 + first)
    cell = target % z
    keep = ((source + ahead - target) % 128 == 0) & (cell >= ahead - RADIUS) & (cell <= ahead + 20)
    return keep.astype(F32).astype(BF)


def toeplitz(rows, high_ref, low_ref, z, depth, rolled):
    groups, tiles = rows.shape[0] // 2, z // 16
    shifts = shift_matrix(z, rolled, tiles - rolled)
    early = lax.broadcasted_iota(jnp.int32, (16, 128), 1) % z < z - 8

    def group(i):
        for half in range(2):
            at = slice(half * 128, half * 128 + 128)

            def place(ref, b, t, tile):
                ref[pl.ds(i * depth + b * z + 16 * t, 16), at] = tile

            firsts = []
            for b in range(TAPS):
                row = jnp.broadcast_to(rows[2 * i + half, b : b + 1, :], (16, 128))
                firsts.append(pltpu.roll(row, 0, 1, stride=1, stride_axis=0))
            for part, ref in zip(split(jnp.concatenate(firsts, axis=0)), (high_ref, low_ref)):
                moved = dot(part, shifts).astype(BF)
                for b in range(TAPS):
                    for t in range(rolled, tiles):
                        lanes = slice(128 * (t - rolled), 128 * (t - rolled) + 128)
                        place(ref, b, t, moved[16 * b : 16 * b + 16, lanes])
            for b in range(TAPS):
                for t in range(rolled):
                    tile = pltpu.roll(firsts[b], 16 * t, 1) if t else jnp.where(early, firsts[b], 0.0)
                    for part, ref in zip(split(tile), (high_ref, low_ref)):
                        place(ref, b, t, part)
        if depth > TAPS * z:
            start = i * depth + TAPS * z
            for ref in (high_ref, low_ref):
                ref[pl.ds(start, depth - TAPS * z), :] = jnp.zeros((depth - TAPS * z, 256), BF)

    for i in range(groups):
        group(i)


def gather_taps(window, high_ref, low_ref, first_plane, first_row, z):
    per = 128 // z

    def pair(p):
        for lane_block in range(high_ref.shape[2] // 128):
            pieces = []
            for q in range(per):
                row = first_row + lane_block * per + q
                pieces.append(window[pl.ds(first_plane + 2 * p, 2), row : row + 8, :])
            value = pieces[0] if per == 1 else jnp.concatenate(pieces, axis=-1)
            high, low = split(value.reshape(16, 128))
            at = slice(lane_block * 128, lane_block * 128 + 128)
            high_ref[p, :, at] = high
            low_ref[p, :, at] = low

    for p in range(high_ref.shape[0]):
        pair(p)


def products(ah, al, wh, wl):
    return dot(ah, wh) + dot(al, wh) + dot(ah, wl)


def small_convolution(high_a, low_a, high_w, low_w, pairs, step, groups, depth, z, planes):
    total = None
    for i in range(groups):
        ah = high_a[i * step : i * step + pairs].reshape(pairs * 16, depth)
        al = low_a[i * step : i * step + pairs].reshape(pairs * 16, depth)
        at = slice(i * depth, (i + 1) * depth)
        part = products(ah, al, high_w[at], low_w[at])
        total = part if total is None else total + part
    total = total.reshape(pairs * 2, 8, 256)
    result = None
    for j in range(256 // z):
        piece = total[j : j + planes, :, j * z : (j + 1) * z]
        result = piece if result is None else result + piece
    return result


def fine_step(i, high_a, low_a, high_w, low_w, total):
    def rows(ref):
        first = ref[pl.ds(2 * i, 25)].reshape(400, 1408)
        second = ref[pl.ds(2 * i + 1, 25)].reshape(400, 1408)
        return jnp.concatenate([first, second], axis=-1)

    at = pl.ds(i * 2816, 2816)
    total[...] += products(rows(high_a), rows(low_a), high_w[at], low_w[at])


def restrict_matrix(z):
    source = lax.broadcasted_iota(jnp.int32, (z, z // 2), 0)
    target = lax.broadcasted_iota(jnp.int32, (z, z // 2), 1)
    away = jnp.abs(source - 2 * target)
    weight = jnp.where(away == 0, 0.75, jnp.where(away == 1, 0.5, jnp.where(away == 2, 0.125, 0.0)))
    return weight.astype(F32).astype(BF)


def prolong_matrix(z):
    source = lax.broadcasted_iota(jnp.int32, (z, 2 * z), 0)
    target = lax.broadcasted_iota(jnp.int32, (z, 2 * z), 1)
    away = jnp.abs(target - 2 * source)
    weight = jnp.where(away == 0, 0.75, jnp.where(away == 1, 0.5, jnp.where(away == 2, 0.125, 0.0)))
    return weight.astype(F32).astype(BF)


def restrict(block, along_x, first_plane, first_row, at, z):
    planes = along_x.shape[0]
    for i in range(planes):
        total = None
        for a, weight in enumerate(SPLINE):
            source = first_plane + 2 * i + a
            if 0 <= source < block.shape[0]:
                piece = weight * block[source]
                total = piece if total is None else total + piece
        along_x[i, at : at + block.shape[1], :] = total
    rows = None
    for b, weight in enumerate(SPLINE):
        piece = weight * along_x[:, pl.ds(first_row + b, 8, stride=2), :]
        rows = piece if rows is None else rows + piece
    result = exact_dot(rows.reshape(planes * 8, z), restrict_matrix(z))
    return result.reshape(planes, 8, z // 2)


def inside(planes, first_x, count_x, first_y, count_y, z):
    x = first_x + lax.broadcasted_iota(jnp.int32, (planes, 8, z), 0)
    y = first_y + lax.broadcasted_iota(jnp.int32, (planes, 8, z), 1)
    return (x >= 0) & (x < count_x) & (y >= 0) & (y < count_y)


def whole(
    nx, ny,
    charge_hbm, kernel_fine_hbm, kernel_mid_hbm, kernel_top_hbm, out,
    charge, kernel_fine, kernel_mid, kernel_top,
    fine, along_fine, middle, along_middle, top,
    padded, rows_f, rows_m, rows_t,
    wfh, wfl, wmh, wml, wth, wtl, afh, afl, amh, aml, ath, atl,
    total, pot_z, pot_y, top_z, top_y, load_sems, send_sems, recv_sems,
):
    gx, gy = lax.axis_index("gx"), lax.axis_index("gy")

    loads = [
        pltpu.make_async_copy(source, target, load_sems.at[n])
        for n, (source, target) in enumerate((
            (charge_hbm, charge), (kernel_mid_hbm, kernel_mid),
            (kernel_top_hbm, kernel_top), (kernel_fine_hbm, kernel_fine),
        ))
    ]
    for load in loads:
        load.start()

    def exists(dx, dy):
        return (gx + dx >= 0) & (gx + dx < nx) & (gy + dy >= 0) & (gy + dy < ny)

    def transfer(number):
        dx, dy, (px, lx), (py, ly), tx, ty = EVERY[number]
        if number < N_FINE:
            source, target = charge, fine.at[pl.ds(tx, lx), pl.ds(ty, ly)]
        else:
            source = middle if number < N_MIDDLE else top
            target = source.at[pl.ds(tx, lx), pl.ds(ty, ly)]
        return pltpu.make_async_remote_copy(
            src_ref=source.at[pl.ds(px, lx), pl.ds(py, ly)], dst_ref=target,
            send_sem=send_sems.at[number], recv_sem=recv_sems.at[number],
            device_id={"gx": gx + dx, "gy": gy + dy},
            device_id_type=pl.DeviceIdType.MESH,
        )

    def start(numbers):
        for number in numbers:
            @pl.when(exists(EVERY[number][0], EVERY[number][1]))
            def _(number=number):
                transfer(number).start()

    def arrive(numbers):
        for number in numbers:
            @pl.when(exists(-EVERY[number][0], -EVERY[number][1]))
            def _(number=number):
                transfer(number).wait_recv()

    def sent(numbers):
        for number in numbers:
            @pl.when(exists(EVERY[number][0], EVERY[number][1]))
            def _(number=number):
                transfer(number).wait_send()

    for ref in (fine, middle, top):
        ref[...] = jnp.zeros_like(ref)

    barrier = pltpu.get_barrier_semaphore()
    for dx in (-1, 0, 1):
        for dy in range(-REACH, REACH + 1):
            if dx == 0 and dy == 0:
                continue
            @pl.when(exists(dx, dy))
            def _(dx=dx, dy=dy):
                pl.semaphore_signal(
                    barrier, inc=1, device_id={"gx": gx + dx, "gy": gy + dy},
                    device_id_type=pl.DeviceIdType.MESH,
                )

    for ref in (along_fine, along_middle):
        ref[...] = jnp.zeros_like(ref)
    for load in loads:
        load.wait()

    fine[FX : FX + 48, FROW : FROW + 8, :] = charge[...]
    base_rows(kernel_mid, padded, rows_m, 64)
    toeplitz(rows_m, wmh, wml, 64, 768, 2)
    base_rows(kernel_top, padded, rows_t, 32)
    toeplitz(rows_t, wth, wtl, 32, 384, 1)
    base_rows(kernel_fine, padded, rows_f, 128)

    across = 1 + (gx > 0).astype(jnp.int32) + (gx < nx - 1).astype(jnp.int32)
    along = 1 + jnp.minimum(gy, REACH) + jnp.minimum(ny - 1 - gy, REACH)
    pl.semaphore_wait(barrier, across * along - 1)

    start(range(N_FINE))
    toeplitz(rows_f, wfh, wfl, 128, 1408, 5)
    arrive(range(N_FINE))

    near = restrict(fine, along_fine, 0, 2, 0, 128)
    near = jnp.where(inside(27, gx * 24 - 2, nx * 24, gy * 4 - 2, ny * 4, 64), near, 0.0)
    middle[MX : MX + 24, 8:12, :] = near[2:26, 2:6, :]
    top[TX : TX + 12, 8:10, :] = restrict(near, along_middle, 0, 8, 8, 64)[:, 0:2, :]
    start(range(N_FINE, COUNT))

    gather_taps(fine, afh, afl, 1, 3, 128)
    total[...] = jnp.zeros_like(total)

    for i in range(3):
        fine_step(i, afh, afl, wfh, wfl, total)

    arrive(range(N_FINE, N_MIDDLE))
    gather_taps(middle, amh, aml, 0, 2, 64)
    arrive(range(N_MIDDLE, COUNT))
    gather_taps(top, ath, atl, 0, 2, 32)
    top_pot = small_convolution(ath, atl, wth, wtl, 11, 4, 2, 384, 32, 15)
    top_pot = jnp.where(inside(15, gx * 12 - 1, nx * 12, gy * 2 - 1, ny * 2, 32), top_pot, 0.0)
    top_z[...] = exact_dot(top_pot.reshape(120, 32), prolong_matrix(32)).reshape(15, 8, 64)
    e0, e1, e2 = top_z[:, 0:3, :], top_z[:, 1:4, :], top_z[:, 2:5, :]
    top_y[...] = jnp.zeros_like(top_y)
    top_y[:, pl.ds(0, 3, stride=2), :] = HALF * e0 + HALF * e1
    top_y[:, pl.ds(1, 3, stride=2), :] = EDGE * e0 + MIDDLE * e1 + EDGE * e2

    mid_pot = small_convolution(amh, aml, wmh, wml, 15, 2, 3, 768, 64, 26)
    pieces = []
    for k in range(13):
        f0, f1, f2 = top_y[k], top_y[k + 1], top_y[k + 2]
        pieces.append((HALF * f0 + HALF * f1)[None])
        pieces.append((EDGE * f0 + MIDDLE * f1 + EDGE * f2)[None])
    mid_pot = mid_pot + jnp.concatenate(pieces, axis=0)
    mid_pot = jnp.where(inside(26, gx * 24 - 1, nx * 24, gy * 4 - 1, ny * 4, 64), mid_pot, 0.0)
    pot_z[...] = exact_dot(mid_pot.reshape(208, 64), prolong_matrix(64)).reshape(26, 8, 128)
    e0, e1, e2 = pot_z[:, 0:4, :], pot_z[:, 1:5, :], pot_z[:, 2:6, :]
    pot_y[:, pl.ds(0, 4, stride=2), :] = EDGE * e0 + MIDDLE * e1 + EDGE * e2
    pot_y[:, pl.ds(1, 4, stride=2), :] = HALF * e1 + HALF * e2

    for m in range(24):
        f0, f1, f2 = pot_y[m], pot_y[m + 1], pot_y[m + 2]
        for odd in range(2):
            x = 2 * m + odd
            near = total[8 * x : 8 * x + 8, 0:128]
            far = total[8 * x + 8 : 8 * x + 16, 128:256]
            fill = HALF * f1 + HALF * f2 if odd else EDGE * f0 + MIDDLE * f1 + EDGE * f2
            out[x] = near + far + fill

    sent(range(COUNT))


def solution(mesh):
    nx, ny = mesh.shape["gx"], mesh.shape["gy"]
    vmem = pltpu.VMEM
    scratch = [
        vmem((48, 8, 128), F32), vmem((11, 11, 11), F32), vmem((11, 11, 11), F32),
        vmem((11, 11, 11), F32),
        vmem((62, 24, 128), F32), vmem((27, 32, 128), F32), vmem((40, 24, 64), F32),
        vmem((12, 32, 64), F32), vmem((32, 24, 32), F32), vmem((16, 16, 128), F32),
        vmem((12, 16, 128), F32), vmem((6, 16, 128), F32), vmem((4, 16, 128), F32),
        vmem((8448, 256), BF), vmem((8448, 256), BF), vmem((2304, 256), BF), vmem((2304, 256), BF),
        vmem((768, 256), BF), vmem((768, 256), BF),
        vmem((30, 16, 1408), BF), vmem((30, 16, 1408), BF), vmem((19, 16, 768), BF),
        vmem((19, 16, 768), BF), vmem((15, 16, 384), BF), vmem((15, 16, 384), BF),
        vmem((400, 256), F32), vmem((26, 8, 128), F32), vmem((26, 8, 128), F32),
        vmem((15, 8, 64), F32), vmem((15, 8, 64), F32),
        pltpu.SemaphoreType.DMA((4,)),
        pltpu.SemaphoreType.DMA((COUNT,)), pltpu.SemaphoreType.DMA((COUNT,)),
    ]

    def shards(charge, kernel_fine, kernel_mid, kernel_top):
        return pl.pallas_call(
            functools.partial(whole, nx, ny),
            out_shape=jax.ShapeDtypeStruct(charge.shape, F32),
            in_specs=[pl.BlockSpec(memory_space=pl.ANY)] * 4,
            out_specs=pl.BlockSpec(memory_space=pltpu.VMEM),
            scratch_shapes=scratch,
            compiler_params=pltpu.CompilerParams(
                collective_id=0, has_side_effects=True, vmem_limit_bytes=60 << 20
            ),
            name="multilevel",
        )(charge, kernel_fine, kernel_mid, kernel_top)

    return jax.shard_map(
        shards, mesh=mesh, in_specs=(P("gx", "gy", None), P(), P(), P()),
        out_specs=P("gx", "gy", None), check_vma=False,
    )
```

```python
import functools

import jax
import jax.numpy as jnp
from jax import lax
from jax.experimental import pallas as pl
from jax.experimental.pallas import tpu as pltpu
from jax.sharding import PartitionSpec as P

BF = jnp.bfloat16
F32 = jnp.float32
SPLINE = (0.125, 0.5, 0.75, 0.5, 0.125)
EDGE, MIDDLE, HALF = 0.125, 0.75, 0.5
TAPS = 11
RADIUS = 5

FX, FROW = 6, 8
MX, TX = 6, 6


def messages():
    fine, middle, top = [], [], []
    for dx in (-1, 0, 1):
        sx = {1: (42, 6), 0: (0, 48), -1: (0, 5)}[dx]
        tx = {1: 0, 0: 6, -1: 54}[dx]
        for dy in (-1, 0, 1):
            sy = {1: (2, 6), 0: (0, 8), -1: (0, 5)}[dy]
            ty = {1: 2, 0: 8, -1: 16}[dy]
            fine.append((dx, dy, sx, sy, tx, ty))
        sx = {1: (24, 6), 0: (6, 24), -1: (6, 6)}[dx]
        tx = {1: 0, 0: 6, -1: 30}[dx]
        for dy in range(-2, 3):
            sy = {2: (10, 2), -2: (8, 2)}.get(dy, (8, 4))
            ty = {2: 2, 1: 4, 0: 8, -1: 12, -2: 16}[dy]
            middle.append((dx, dy, sx, sy, tx, ty))
        sx = {1: (12, 6), 0: (6, 12), -1: (6, 7)}[dx]
        tx = {1: 0, 0: 6, -1: 18}[dx]
        for dy in range(-4, 4):
            top.append((dx, dy, sx, (8, 2), tx, 8 - 2 * dy))
    return [[m for m in group if m[:2] != (0, 0)] for group in (fine, middle, top)]


FINE, MIDDLE_MSG, TOP = messages()
EVERY = FINE + MIDDLE_MSG + TOP
COUNT = len(EVERY)
N_FINE = len(FINE)
N_MIDDLE = N_FINE + len(MIDDLE_MSG)


def split(value):
    high = value.astype(BF)
    return high, (value - high.astype(F32)).astype(BF)


def dot(a, b):
    return jnp.dot(a, b, preferred_element_type=F32)


def exact_dot(value, weights):
    high, low = split(value)
    return dot(high, weights) + dot(low, weights)


def base_rows(kernel_ref, padded, rows, z):
    per = 128 // z
    padded[...] = jnp.zeros_like(padded)
    padded[0:TAPS, 0:TAPS, 0:TAPS] = kernel_ref[...]
    tap = lax.broadcasted_iota(jnp.int32, (128, per * 128), 0)
    lane = lax.broadcasted_iota(jnp.int32, (128, per * 128), 1)
    place = (lane // 128) * z + RADIUS - tap
    spread = ((lane - place) % 128 == 0) & (tap < TAPS)
    spread = spread.astype(F32).astype(BF)
    table = exact_dot(padded[...].reshape(256, 128), spread).reshape(16, 16, per * 128)
    for n in range(rows.shape[0]):
        total = None
        for q in range(per):
            piece = table[n * per + q, :, q * 128 : (q + 1) * 128]
            total = piece if total is None else total + piece
        rows[n] = total


def shift_matrix(z, first, tiles):
    source = lax.broadcasted_iota(jnp.int32, (128, tiles * 128), 0)
    target = lax.broadcasted_iota(jnp.int32, (128, tiles * 128), 1)
    ahead = 16 * (target // 128 + first)
    cell = target % z
    keep = ((source + ahead - target) % 128 == 0) & (cell >= ahead - RADIUS) & (cell <= ahead + 20)
    return keep.astype(F32).astype(BF)


def toeplitz(rows, high_ref, low_ref, z, depth, rolled):
    groups, tiles = rows.shape[0] // 2, z // 16
    shifts = shift_matrix(z, rolled, tiles - rolled)
    early = lax.broadcasted_iota(jnp.int32, (16, 128), 1) % z < z - 8

    def group(i):
        for half in range(2):
            at = slice(half * 128, half * 128 + 128)

            def place(ref, b, t, tile):
                ref[pl.ds(i * depth + b * z + 16 * t, 16), at] = tile

            firsts = []
            for b in range(TAPS):
                row = jnp.broadcast_to(rows[2 * i + half, b : b + 1, :], (16, 128))
                firsts.append(pltpu.roll(row, 0, 1, stride=1, stride_axis=0))
            for part, ref in zip(split(jnp.concatenate(firsts, axis=0)), (high_ref, low_ref)):
                moved = dot(part, shifts).astype(BF)
                for b in range(TAPS):
                    for t in range(rolled, tiles):
                        lanes = slice(128 * (t - rolled), 128 * (t - rolled) + 128)
                        place(ref, b, t, moved[16 * b : 16 * b + 16, lanes])
            for b in range(TAPS):
                for t in range(rolled):
                    tile = pltpu.roll(firsts[b], 16 * t, 1) if t else jnp.where(early, firsts[b], 0.0)
                    for part, ref in zip(split(tile), (high_ref, low_ref)):
                        place(ref, b, t, part)
        if depth > TAPS * z:
            start = i * depth + TAPS * z
            for ref in (high_ref, low_ref):
                ref[pl.ds(start, depth - TAPS * z), :] = jnp.zeros((depth - TAPS * z, 256), BF)

    for i in range(groups):
        group(i)


def gather_taps(window, high_ref, low_ref, first_plane, first_row, z):
    per = 128 // z

    def pair(p):
        for lane_block in range(high_ref.shape[2] // 128):
            pieces = []
            for q in range(per):
                row = first_row + lane_block * per + q
                pieces.append(window[pl.ds(first_plane + 2 * p, 2), row : row + 8, :])
            value = pieces[0] if per == 1 else jnp.concatenate(pieces, axis=-1)
            high, low = split(value.reshape(16, 128))
            at = slice(lane_block * 128, lane_block * 128 + 128)
            high_ref[p, :, at] = high
            low_ref[p, :, at] = low

    for p in range(high_ref.shape[0]):
        pair(p)


def products(ah, al, wh, wl):
    return dot(ah, wh) + dot(al, wh) + dot(ah, wl)


def small_convolution(high_a, low_a, high_w, low_w, pairs, step, groups, depth, z, planes):
    total = None
    for i in range(groups):
        ah = high_a[i * step : i * step + pairs].reshape(pairs * 16, depth)
        al = low_a[i * step : i * step + pairs].reshape(pairs * 16, depth)
        at = slice(i * depth, (i + 1) * depth)
        part = products(ah, al, high_w[at], low_w[at])
        total = part if total is None else total + part
    total = total.reshape(pairs * 2, 8, 256)
    result = None
    for j in range(256 // z):
        piece = total[j : j + planes, :, j * z : (j + 1) * z]
        result = piece if result is None else result + piece
    return result


def fine_step(i, high_a, low_a, high_w, low_w, total):
    def rows(ref):
        first = ref[pl.ds(2 * i, 25)].reshape(400, 1408)
        second = ref[pl.ds(2 * i + 1, 25)].reshape(400, 1408)
        return jnp.concatenate([first, second], axis=-1)

    at = pl.ds(i * 2816, 2816)
    total[...] += products(rows(high_a), rows(low_a), high_w[at], low_w[at])


def restrict_matrix(z):
    source = lax.broadcasted_iota(jnp.int32, (z, z // 2), 0)
    target = lax.broadcasted_iota(jnp.int32, (z, z // 2), 1)
    away = jnp.abs(source - 2 * target)
    weight = jnp.where(away == 0, 0.75, jnp.where(away == 1, 0.5, jnp.where(away == 2, 0.125, 0.0)))
    return weight.astype(F32).astype(BF)


def prolong_matrix(z):
    source = lax.broadcasted_iota(jnp.int32, (z, 2 * z), 0)
    target = lax.broadcasted_iota(jnp.int32, (z, 2 * z), 1)
    away = jnp.abs(target - 2 * source)
    weight = jnp.where(away == 0, 0.75, jnp.where(away == 1, 0.5, jnp.where(away == 2, 0.125, 0.0)))
    return weight.astype(F32).astype(BF)


def restrict(block, along_x, first_plane, first_row, at, z):
    planes = along_x.shape[0]
    for i in range(planes):
        total = None
        for a, weight in enumerate(SPLINE):
            source = first_plane + 2 * i + a
            if 0 <= source < block.shape[0]:
                piece = weight * block[source]
                total = piece if total is None else total + piece
        along_x[i, at : at + block.shape[1], :] = total
    rows = None
    for b, weight in enumerate(SPLINE):
        piece = weight * along_x[:, pl.ds(first_row + b, 8, stride=2), :]
        rows = piece if rows is None else rows + piece
    result = exact_dot(rows.reshape(planes * 8, z), restrict_matrix(z))
    return result.reshape(planes, 8, z // 2)


def inside(planes, first_x, count_x, first_y, count_y, z):
    x = first_x + lax.broadcasted_iota(jnp.int32, (planes, 8, z), 0)
    y = first_y + lax.broadcasted_iota(jnp.int32, (planes, 8, z), 1)
    return (x >= 0) & (x < count_x) & (y >= 0) & (y < count_y)


def whole(
    nx, ny,
    charge_hbm, kernel_fine_hbm, kernel_mid_hbm, kernel_top_hbm, out,
    charge, kernel_fine, kernel_mid, kernel_top,
    fine, along_fine, middle, along_middle, top,
    padded, rows_f, rows_m, rows_t,
    wfh, wfl, wmh, wml, wth, wtl, afh, afl, amh, aml, ath, atl,
    total, pot_z, pot_y, top_z, top_y, load_sems, send_sems, recv_sems,
    near_sem, far_sem,
):
    gx, gy = lax.axis_index("gx"), lax.axis_index("gy")

    loads = [
        pltpu.make_async_copy(source, target, load_sems.at[n])
        for n, (source, target) in enumerate((
            (charge_hbm, charge), (kernel_mid_hbm, kernel_mid),
            (kernel_top_hbm, kernel_top), (kernel_fine_hbm, kernel_fine),
        ))
    ]
    for load in loads:
        load.start()

    def exists(dx, dy):
        return (gx + dx >= 0) & (gx + dx < nx) & (gy + dy >= 0) & (gy + dy < ny)

    def transfer(number):
        dx, dy, (px, lx), (py, ly), tx, ty = EVERY[number]
        if number < N_FINE:
            source, target = charge, fine.at[pl.ds(tx, lx), pl.ds(ty, ly)]
        else:
            source = middle if number < N_MIDDLE else top
            target = source.at[pl.ds(tx, lx), pl.ds(ty, ly)]
        return pltpu.make_async_remote_copy(
            src_ref=source.at[pl.ds(px, lx), pl.ds(py, ly)], dst_ref=target,
            send_sem=send_sems.at[number], recv_sem=recv_sems.at[number],
            device_id={"gx": gx + dx, "gy": gy + dy},
            device_id_type=pl.DeviceIdType.MESH,
        )

    def start(numbers):
        for number in numbers:
            @pl.when(exists(EVERY[number][0], EVERY[number][1]))
            def _(number=number):
                transfer(number).start()

    def arrive(numbers):
        for number in numbers:
            @pl.when(exists(-EVERY[number][0], -EVERY[number][1]))
            def _(number=number):
                transfer(number).wait_recv()

    def sent(numbers):
        for number in numbers:
            @pl.when(exists(EVERY[number][0], EVERY[number][1]))
            def _(number=number):
                transfer(number).wait_send()

    for ref in (fine, middle, top):
        ref[...] = jnp.zeros_like(ref)

    def greet(semaphore, reach):
        for dx in (-1, 0, 1):
            for dy in range(-reach, reach + 1):
                if dx == 0 and dy == 0:
                    continue
                @pl.when(exists(dx, dy))
                def _(dx=dx, dy=dy):
                    pl.semaphore_signal(
                        semaphore, inc=1, device_id={"gx": gx + dx, "gy": gy + dy},
                        device_id_type=pl.DeviceIdType.MESH,
                    )

    def greeted(semaphore, reach):
        across = 1 + (gx > 0).astype(jnp.int32) + (gx < nx - 1).astype(jnp.int32)
        along = 1 + jnp.minimum(gy, reach) + jnp.minimum(ny - 1 - gy, reach)
        pl.semaphore_wait(semaphore, across * along - 1)

    barrier = pltpu.get_barrier_semaphore()
    greet(barrier, 1)

    for ref in (along_fine, along_middle):
        ref[...] = jnp.zeros_like(ref)
    for load in loads:
        load.wait()

    fine[FX : FX + 48, FROW : FROW + 8, :] = charge[...]
    base_rows(kernel_mid, padded, rows_m, 64)
    toeplitz(rows_m, wmh, wml, 64, 768, 2)
    base_rows(kernel_fine, padded, rows_f, 128)

    greeted(barrier, 1)
    start(range(N_FINE))
    greet(near_sem, 1)
    toeplitz(rows_f, wfh, wfl, 128, 1408, 5)
    greeted(near_sem, 1)
    greet(far_sem, 2)
    base_rows(kernel_top, padded, rows_t, 32)
    toeplitz(rows_t, wth, wtl, 32, 384, 1)
    arrive(range(N_FINE))

    near = restrict(fine, along_fine, 0, 2, 0, 128)
    near = jnp.where(inside(27, gx * 24 - 2, nx * 24, gy * 4 - 2, ny * 4, 64), near, 0.0)
    middle[MX : MX + 24, 8:12, :] = near[2:26, 2:6, :]
    top[TX : TX + 12, 8:10, :] = restrict(near, along_middle, 0, 8, 8, 64)[:, 0:2, :]
    start(range(N_FINE, N_MIDDLE))
    greeted(far_sem, 2)
    start(range(N_MIDDLE, COUNT))

    gather_taps(fine, afh, afl, 1, 3, 128)
    total[...] = jnp.zeros_like(total)

    for i in range(2):
        fine_step(i, afh, afl, wfh, wfl, total)

    arrive(range(N_FINE, COUNT))
    gather_taps(middle, amh, aml, 0, 2, 64)
    gather_taps(top, ath, atl, 0, 2, 32)
    fine_step(2, afh, afl, wfh, wfl, total)
    top_pot = small_convolution(ath, atl, wth, wtl, 11, 4, 2, 384, 32, 15)
    top_pot = jnp.where(inside(15, gx * 12 - 1, nx * 12, gy * 2 - 1, ny * 2, 32), top_pot, 0.0)
    top_z[...] = exact_dot(top_pot.reshape(120, 32), prolong_matrix(32)).reshape(15, 8, 64)
    e0, e1, e2 = top_z[:, 0:3, :], top_z[:, 1:4, :], top_z[:, 2:5, :]
    top_y[...] = jnp.zeros_like(top_y)
    top_y[:, pl.ds(0, 3, stride=2), :] = HALF * e0 + HALF * e1
    top_y[:, pl.ds(1, 3, stride=2), :] = EDGE * e0 + MIDDLE * e1 + EDGE * e2

    mid_pot = small_convolution(amh, aml, wmh, wml, 15, 2, 3, 768, 64, 26)
    pieces = []
    for k in range(13):
        f0, f1, f2 = top_y[k], top_y[k + 1], top_y[k + 2]
        pieces.append((HALF * f0 + HALF * f1)[None])
        pieces.append((EDGE * f0 + MIDDLE * f1 + EDGE * f2)[None])
    mid_pot = mid_pot + jnp.concatenate(pieces, axis=0)
    mid_pot = jnp.where(inside(26, gx * 24 - 1, nx * 24, gy * 4 - 1, ny * 4, 64), mid_pot, 0.0)
    pot_z[...] = exact_dot(mid_pot.reshape(208, 64), prolong_matrix(64)).reshape(26, 8, 128)
    e0, e1, e2 = pot_z[:, 0:4, :], pot_z[:, 1:5, :], pot_z[:, 2:6, :]
    pot_y[:, pl.ds(0, 4, stride=2), :] = EDGE * e0 + MIDDLE * e1 + EDGE * e2
    pot_y[:, pl.ds(1, 4, stride=2), :] = HALF * e1 + HALF * e2

    for m in range(24):
        f0, f1, f2 = pot_y[m], pot_y[m + 1], pot_y[m + 2]
        for odd in range(2):
            x = 2 * m + odd
            near = total[8 * x : 8 * x + 8, 0:128]
            far = total[8 * x + 8 : 8 * x + 16, 128:256]
            fill = HALF * f1 + HALF * f2 if odd else EDGE * f0 + MIDDLE * f1 + EDGE * f2
            out[x] = near + far + fill

    sent(range(COUNT))


def solution(mesh):
    nx, ny = mesh.shape["gx"], mesh.shape["gy"]
    vmem = pltpu.VMEM
    scratch = [
        vmem((48, 8, 128), F32), vmem((11, 11, 11), F32), vmem((11, 11, 11), F32),
        vmem((11, 11, 11), F32),
        vmem((62, 24, 128), F32), vmem((27, 32, 128), F32), vmem((40, 24, 64), F32),
        vmem((12, 32, 64), F32), vmem((32, 24, 32), F32), vmem((16, 16, 128), F32),
        vmem((12, 16, 128), F32), vmem((6, 16, 128), F32), vmem((4, 16, 128), F32),
        vmem((8448, 256), BF), vmem((8448, 256), BF), vmem((2304, 256), BF), vmem((2304, 256), BF),
        vmem((768, 256), BF), vmem((768, 256), BF),
        vmem((30, 16, 1408), BF), vmem((30, 16, 1408), BF), vmem((19, 16, 768), BF),
        vmem((19, 16, 768), BF), vmem((15, 16, 384), BF), vmem((15, 16, 384), BF),
        vmem((400, 256), F32), vmem((26, 8, 128), F32), vmem((26, 8, 128), F32),
        vmem((15, 8, 64), F32), vmem((15, 8, 64), F32),
        pltpu.SemaphoreType.DMA((4,)),
        pltpu.SemaphoreType.DMA((COUNT,)), pltpu.SemaphoreType.DMA((COUNT,)),
        pltpu.SemaphoreType.REGULAR, pltpu.SemaphoreType.REGULAR,
    ]

    def shards(charge, kernel_fine, kernel_mid, kernel_top):
        return pl.pallas_call(
            functools.partial(whole, nx, ny),
            out_shape=jax.ShapeDtypeStruct(charge.shape, F32),
            in_specs=[pl.BlockSpec(memory_space=pl.ANY)] * 4,
            out_specs=pl.BlockSpec(memory_space=pltpu.VMEM),
            scratch_shapes=scratch,
            compiler_params=pltpu.CompilerParams(
                collective_id=0, has_side_effects=True, vmem_limit_bytes=60 << 20
            ),
            name="multilevel",
        )(charge, kernel_fine, kernel_mid, kernel_top)

    return jax.shard_map(
        shards, mesh=mesh, in_specs=(P("gx", "gy", None), P(), P(), P()),
        out_specs=P("gx", "gy", None), check_vma=False,
    )
```

```python
import functools

import jax
import jax.numpy as jnp
from jax import lax
from jax.experimental import pallas as pl
from jax.experimental.pallas import tpu as pltpu
from jax.sharding import PartitionSpec as P

BF = jnp.bfloat16
F32 = jnp.float32
SPLINE = (0.125, 0.5, 0.75, 0.5, 0.125)
EDGE, MIDDLE, HALF = 0.125, 0.75, 0.5
TAPS = 11
RADIUS = 5

FX, FROW = 6, 8
MX, TX = 3, 2


def messages():
    fine, middle, top = [], [], []
    for dx in (-1, 0, 1):
        sx = {1: (42, 6), 0: (0, 48), -1: (0, 5)}[dx]
        tx = {1: 0, 0: 6, -1: 54}[dx]
        for dy in (-1, 0, 1):
            sy = {1: (2, 6), 0: (0, 8), -1: (0, 5)}[dy]
            ty = {1: 2, 0: 8, -1: 16}[dy]
            fine.append((dx, dy, sx, sy, tx, ty))
        sx = {1: (12, 3), 0: (3, 12), -1: (3, 3)}[dx]
        tx = {1: 0, 0: 3, -1: 15}[dx]
        for dy in range(-2, 3):
            sy = {2: (10, 2), -2: (8, 2)}.get(dy, (8, 4))
            ty = {2: 2, 1: 4, 0: 8, -1: 12, -2: 16}[dy]
            middle.append((dx, dy, sx, sy, tx, ty))
        sx = {1: (3, 2), 0: (2, 3), -1: (2, 2)}[dx]
        tx = {1: 0, 0: 2, -1: 5}[dx]
        for dy in range(-4, 4):
            top.append((dx, dy, sx, (8, 2), tx, 8 - 2 * dy))
    return [[m for m in group if m[:2] != (0, 0)] for group in (fine, middle, top)]


FINE, MIDDLE_MSG, TOP = messages()
EVERY = FINE + MIDDLE_MSG + TOP
COUNT = len(EVERY)
N_FINE = len(FINE)
N_MIDDLE = N_FINE + len(MIDDLE_MSG)


def split(value):
    high = value.astype(BF)
    return high, (value - high.astype(F32)).astype(BF)


def dot(a, b):
    return jnp.dot(a, b, preferred_element_type=F32)


def exact_dot(value, weights):
    high, low = split(value)
    return dot(high, weights) + dot(low, weights)


def base_rows(kernel_ref, padded, rows, z):
    per = 128 // z
    padded[...] = jnp.zeros_like(padded)
    padded[0:TAPS, 0:TAPS, 0:TAPS] = kernel_ref[...]
    tap = lax.broadcasted_iota(jnp.int32, (128, per * 128), 0)
    lane = lax.broadcasted_iota(jnp.int32, (128, per * 128), 1)
    place = (lane // 128) * z + RADIUS - tap
    spread = ((lane - place) % 128 == 0) & (tap < TAPS)
    spread = spread.astype(F32).astype(BF)
    table = exact_dot(padded[...].reshape(256, 128), spread).reshape(16, 16, per * 128)
    for n in range(rows.shape[0]):
        total = None
        for q in range(per):
            piece = table[n * per + q, :, q * 128 : (q + 1) * 128]
            total = piece if total is None else total + piece
        rows[n] = total


def shift_matrix(z, first, tiles):
    source = lax.broadcasted_iota(jnp.int32, (128, tiles * 128), 0)
    target = lax.broadcasted_iota(jnp.int32, (128, tiles * 128), 1)
    ahead = 16 * (target // 128 + first)
    cell = target % z
    keep = ((source + ahead - target) % 128 == 0) & (cell >= ahead - RADIUS) & (cell <= ahead + 20)
    return keep.astype(F32).astype(BF)


def toeplitz(rows, high_ref, low_ref, z, depth, rolled):
    groups, tiles = rows.shape[0] // 2, z // 16
    shifts = shift_matrix(z, rolled, tiles - rolled)
    early = lax.broadcasted_iota(jnp.int32, (16, 128), 1) % z < z - 8

    def group(i):
        for half in range(2):
            at = slice(half * 128, half * 128 + 128)

            def place(ref, b, t, tile):
                ref[pl.ds(i * depth + b * z + 16 * t, 16), at] = tile

            firsts = []
            for b in range(TAPS):
                row = jnp.broadcast_to(rows[2 * i + half, b : b + 1, :], (16, 128))
                firsts.append(pltpu.roll(row, 0, 1, stride=1, stride_axis=0))
            for part, ref in zip(split(jnp.concatenate(firsts, axis=0)), (high_ref, low_ref)):
                moved = dot(part, shifts).astype(BF)
                for b in range(TAPS):
                    for t in range(rolled, tiles):
                        lanes = slice(128 * (t - rolled), 128 * (t - rolled) + 128)
                        place(ref, b, t, moved[16 * b : 16 * b + 16, lanes])
            for b in range(TAPS):
                for t in range(rolled):
                    tile = pltpu.roll(firsts[b], 16 * t, 1) if t else jnp.where(early, firsts[b], 0.0)
                    for part, ref in zip(split(tile), (high_ref, low_ref)):
                        place(ref, b, t, part)
        if depth > TAPS * z:
            start = i * depth + TAPS * z
            for ref in (high_ref, low_ref):
                ref[pl.ds(start, depth - TAPS * z), :] = jnp.zeros((depth - TAPS * z, 256), BF)

    for i in range(groups):
        group(i)


def pack(planes, z):
    per = 128 // z
    groups = [
        jnp.concatenate([planes[per * g + q] for q in range(per)], axis=-1)[None]
        for g in range(planes.shape[0] // per)
    ]
    return jnp.concatenate(groups, axis=0)


def gather_taps(window, high_ref, low_ref, first_plane, first_row, z):
    per = 128 // z
    for p in range(high_ref.shape[0]):
        for lane_block in range(high_ref.shape[2] // 128):
            planes = []
            for plane in (first_plane + 2 * p, first_plane + 2 * p + 1):
                row, at = first_row + lane_block * per, plane % per * z
                pieces = [window[plane // per, row + q : row + q + 8, at : at + z] for q in range(per)]
                planes.append(pieces[0] if per == 1 else jnp.concatenate(pieces, axis=-1))
            high, low = split(jnp.concatenate(planes, axis=0))
            at = slice(lane_block * 128, lane_block * 128 + 128)
            high_ref[p, :, at] = high
            low_ref[p, :, at] = low


def products(ah, al, wh, wl):
    return dot(ah, wh) + dot(al, wh) + dot(ah, wl)


def small_convolution(high_a, low_a, high_w, low_w, pairs, step, groups, depth, z, planes):
    total = None
    for i in range(groups):
        ah = high_a[i * step : i * step + pairs].reshape(pairs * 16, depth)
        al = low_a[i * step : i * step + pairs].reshape(pairs * 16, depth)
        at = slice(i * depth, (i + 1) * depth)
        part = products(ah, al, high_w[at], low_w[at])
        total = part if total is None else total + part
    total = total.reshape(pairs * 2, 8, 256)
    result = None
    for j in range(256 // z):
        piece = total[j : j + planes, :, j * z : (j + 1) * z]
        result = piece if result is None else result + piece
    return result


def fine_step(i, high_a, low_a, high_w, low_w, total):
    def rows(ref):
        first = ref[pl.ds(2 * i, 25)].reshape(400, 1408)
        second = ref[pl.ds(2 * i + 1, 25)].reshape(400, 1408)
        return jnp.concatenate([first, second], axis=-1)

    at = pl.ds(i * 2816, 2816)
    total[...] += products(rows(high_a), rows(low_a), high_w[at], low_w[at])


def restrict_matrix(z):
    source = lax.broadcasted_iota(jnp.int32, (z, z // 2), 0)
    target = lax.broadcasted_iota(jnp.int32, (z, z // 2), 1)
    away = jnp.abs(source - 2 * target)
    weight = jnp.where(away == 0, 0.75, jnp.where(away == 1, 0.5, jnp.where(away == 2, 0.125, 0.0)))
    return weight.astype(F32).astype(BF)


def prolong_matrix(z):
    source = lax.broadcasted_iota(jnp.int32, (z, 2 * z), 0)
    target = lax.broadcasted_iota(jnp.int32, (z, 2 * z), 1)
    away = jnp.abs(target - 2 * source)
    weight = jnp.where(away == 0, 0.75, jnp.where(away == 1, 0.5, jnp.where(away == 2, 0.125, 0.0)))
    return weight.astype(F32).astype(BF)


def restrict(block, along_x, first_plane, first_row, at, z):
    planes = along_x.shape[0]
    for i in range(planes):
        total = None
        for a, weight in enumerate(SPLINE):
            source = first_plane + 2 * i + a
            if 0 <= source < block.shape[0]:
                piece = weight * block[source]
                total = piece if total is None else total + piece
        along_x[i, at : at + block.shape[1], :] = total
    rows = None
    for b, weight in enumerate(SPLINE):
        piece = weight * along_x[:, pl.ds(first_row + b, 8, stride=2), :]
        rows = piece if rows is None else rows + piece
    result = exact_dot(rows.reshape(planes * 8, z), restrict_matrix(z))
    return result.reshape(planes, 8, z // 2)


def inside(planes, first_x, count_x, first_y, count_y, z):
    x = first_x + lax.broadcasted_iota(jnp.int32, (planes, 8, z), 0)
    y = first_y + lax.broadcasted_iota(jnp.int32, (planes, 8, z), 1)
    return (x >= 0) & (x < count_x) & (y >= 0) & (y < count_y)


def whole(
    nx, ny,
    charge_hbm, kernel_fine_hbm, kernel_mid_hbm, kernel_top_hbm, out,
    charge, kernel_fine, kernel_mid, kernel_top,
    fine, along_fine, middle, along_middle, top,
    padded, rows_f, rows_m, rows_t,
    wfh, wfl, wmh, wml, wth, wtl, afh, afl, amh, aml, ath, atl,
    total, pot_z, pot_y, top_z, top_y, load_sems, send_sems, recv_sems,
    near_sem, far_sem,
):
    gx, gy = lax.axis_index("gx"), lax.axis_index("gy")

    loads = [
        pltpu.make_async_copy(source, target, load_sems.at[n])
        for n, (source, target) in enumerate((
            (charge_hbm, charge), (kernel_mid_hbm, kernel_mid),
            (kernel_top_hbm, kernel_top), (kernel_fine_hbm, kernel_fine),
        ))
    ]
    for load in loads:
        load.start()

    def exists(dx, dy):
        return (gx + dx >= 0) & (gx + dx < nx) & (gy + dy >= 0) & (gy + dy < ny)

    def transfer(number):
        dx, dy, (px, lx), (py, ly), tx, ty = EVERY[number]
        if number < N_FINE:
            source, target = charge, fine.at[pl.ds(tx, lx), pl.ds(ty, ly)]
        else:
            source = middle if number < N_MIDDLE else top
            target = source.at[pl.ds(tx, lx), pl.ds(ty, ly)]
        return pltpu.make_async_remote_copy(
            src_ref=source.at[pl.ds(px, lx), pl.ds(py, ly)], dst_ref=target,
            send_sem=send_sems.at[number], recv_sem=recv_sems.at[number],
            device_id={"gx": gx + dx, "gy": gy + dy},
            device_id_type=pl.DeviceIdType.MESH,
        )

    def start(numbers):
        for number in numbers:
            @pl.when(exists(EVERY[number][0], EVERY[number][1]))
            def _(number=number):
                transfer(number).start()

    def arrive(numbers):
        for number in numbers:
            @pl.when(exists(-EVERY[number][0], -EVERY[number][1]))
            def _(number=number):
                transfer(number).wait_recv()

    def sent(numbers):
        for number in numbers:
            @pl.when(exists(EVERY[number][0], EVERY[number][1]))
            def _(number=number):
                transfer(number).wait_send()

    for ref in (fine, middle, top):
        ref[...] = jnp.zeros_like(ref)

    def greet(semaphore, reach):
        for dx in (-1, 0, 1):
            for dy in range(-reach, reach + 1):
                if dx == 0 and dy == 0:
                    continue
                @pl.when(exists(dx, dy))
                def _(dx=dx, dy=dy):
                    pl.semaphore_signal(
                        semaphore, inc=1, device_id={"gx": gx + dx, "gy": gy + dy},
                        device_id_type=pl.DeviceIdType.MESH,
                    )

    def greeted(semaphore, reach):
        across = 1 + (gx > 0).astype(jnp.int32) + (gx < nx - 1).astype(jnp.int32)
        along = 1 + jnp.minimum(gy, reach) + jnp.minimum(ny - 1 - gy, reach)
        pl.semaphore_wait(semaphore, across * along - 1)

    barrier = pltpu.get_barrier_semaphore()
    greet(barrier, 1)

    for ref in (along_fine, along_middle):
        ref[...] = jnp.zeros_like(ref)
    for load in loads:
        load.wait()

    fine[FX : FX + 48, FROW : FROW + 8, :] = charge[...]
    base_rows(kernel_mid, padded, rows_m, 64)
    toeplitz(rows_m, wmh, wml, 64, 768, 2)
    base_rows(kernel_fine, padded, rows_f, 128)

    greeted(barrier, 1)
    start(range(N_FINE))
    greet(near_sem, 1)
    toeplitz(rows_f, wfh, wfl, 128, 1408, 5)
    greeted(near_sem, 1)
    greet(far_sem, 2)
    base_rows(kernel_top, padded, rows_t, 32)
    toeplitz(rows_t, wth, wtl, 32, 384, 1)
    arrive(range(N_FINE))

    near = restrict(fine, along_fine, 0, 2, 0, 128)
    near = jnp.where(inside(27, gx * 24 - 2, nx * 24, gy * 4 - 2, ny * 4, 64), near, 0.0)
    middle[MX : MX + 12, 8:12, :] = pack(near[2:26], 64)[:, 2:6, :]
    top[TX : TX + 3, 8:10, :] = pack(restrict(near, along_middle, 0, 8, 8, 64), 32)[:, 0:2, :]
    start(range(N_FINE, N_MIDDLE))
    greeted(far_sem, 2)
    start(range(N_MIDDLE, COUNT))

    gather_taps(fine, afh, afl, 1, 3, 128)
    total[...] = jnp.zeros_like(total)

    for i in range(2):
        fine_step(i, afh, afl, wfh, wfl, total)

    arrive(range(N_FINE, COUNT))
    gather_taps(middle, amh, aml, 0, 2, 64)
    gather_taps(top, ath, atl, 2, 2, 32)
    fine_step(2, afh, afl, wfh, wfl, total)
    top_pot = small_convolution(ath, atl, wth, wtl, 11, 4, 2, 384, 32, 15)
    top_pot = jnp.where(inside(15, gx * 12 - 1, nx * 12, gy * 2 - 1, ny * 2, 32), top_pot, 0.0)
    top_z[...] = exact_dot(top_pot.reshape(120, 32), prolong_matrix(32)).reshape(15, 8, 64)
    e0, e1, e2 = top_z[:, 0:3, :], top_z[:, 1:4, :], top_z[:, 2:5, :]
    top_y[...] = jnp.zeros_like(top_y)
    top_y[:, pl.ds(0, 3, stride=2), :] = HALF * e0 + HALF * e1
    top_y[:, pl.ds(1, 3, stride=2), :] = EDGE * e0 + MIDDLE * e1 + EDGE * e2

    mid_pot = small_convolution(amh, aml, wmh, wml, 15, 2, 3, 768, 64, 26)
    pieces = []
    for k in range(13):
        f0, f1, f2 = top_y[k], top_y[k + 1], top_y[k + 2]
        pieces.append((HALF * f0 + HALF * f1)[None])
        pieces.append((EDGE * f0 + MIDDLE * f1 + EDGE * f2)[None])
    mid_pot = mid_pot + jnp.concatenate(pieces, axis=0)
    mid_pot = jnp.where(inside(26, gx * 24 - 1, nx * 24, gy * 4 - 1, ny * 4, 64), mid_pot, 0.0)
    pot_z[...] = exact_dot(mid_pot.reshape(208, 64), prolong_matrix(64)).reshape(26, 8, 128)
    e0, e1, e2 = pot_z[:, 0:4, :], pot_z[:, 1:5, :], pot_z[:, 2:6, :]
    pot_y[:, pl.ds(0, 4, stride=2), :] = EDGE * e0 + MIDDLE * e1 + EDGE * e2
    pot_y[:, pl.ds(1, 4, stride=2), :] = HALF * e1 + HALF * e2

    for m in range(24):
        f0, f1, f2 = pot_y[m], pot_y[m + 1], pot_y[m + 2]
        for odd in range(2):
            x = 2 * m + odd
            near = total[8 * x : 8 * x + 8, 0:128]
            far = total[8 * x + 8 : 8 * x + 16, 128:256]
            fill = HALF * f1 + HALF * f2 if odd else EDGE * f0 + MIDDLE * f1 + EDGE * f2
            out[x] = near + far + fill

    sent(range(COUNT))


def solution(mesh):
    nx, ny = mesh.shape["gx"], mesh.shape["gy"]
    vmem = pltpu.VMEM
    scratch = [
        vmem((48, 8, 128), F32), vmem((11, 11, 11), F32), vmem((11, 11, 11), F32),
        vmem((11, 11, 11), F32),
        vmem((62, 24, 128), F32), vmem((27, 32, 128), F32), vmem((20, 24, 128), F32),
        vmem((12, 32, 64), F32), vmem((8, 24, 128), F32), vmem((16, 16, 128), F32),
        vmem((12, 16, 128), F32), vmem((6, 16, 128), F32), vmem((4, 16, 128), F32),
        vmem((8448, 256), BF), vmem((8448, 256), BF), vmem((2304, 256), BF), vmem((2304, 256), BF),
        vmem((768, 256), BF), vmem((768, 256), BF),
        vmem((30, 16, 1408), BF), vmem((30, 16, 1408), BF), vmem((19, 16, 768), BF),
        vmem((19, 16, 768), BF), vmem((15, 16, 384), BF), vmem((15, 16, 384), BF),
        vmem((400, 256), F32), vmem((26, 8, 128), F32), vmem((26, 8, 128), F32),
        vmem((15, 8, 64), F32), vmem((15, 8, 64), F32),
        pltpu.SemaphoreType.DMA((4,)),
        pltpu.SemaphoreType.DMA((COUNT,)), pltpu.SemaphoreType.DMA((COUNT,)),
        pltpu.SemaphoreType.REGULAR, pltpu.SemaphoreType.REGULAR,
    ]

    def shards(charge, kernel_fine, kernel_mid, kernel_top):
        return pl.pallas_call(
            functools.partial(whole, nx, ny),
            out_shape=jax.ShapeDtypeStruct(charge.shape, F32),
            in_specs=[pl.BlockSpec(memory_space=pl.ANY)] * 4,
            out_specs=pl.BlockSpec(memory_space=pltpu.VMEM),
            scratch_shapes=scratch,
            compiler_params=pltpu.CompilerParams(
                collective_id=0, has_side_effects=True, vmem_limit_bytes=60 << 20
            ),
            name="multilevel",
        )(charge, kernel_fine, kernel_mid, kernel_top)

    return jax.shard_map(
        shards, mesh=mesh, in_specs=(P("gx", "gy", None), P(), P(), P()),
        out_specs=P("gx", "gy", None), check_vma=False,
    )
```
